32 devices in a mesh: rep: 16 (over z, y, core), grp: 2 (over x).
Axes of the slice: x: 2, y: 2, z: 4, core: 2. Of those that a mesh axis runs over, the one named last changes fastest.
Arguments:
- tokens: bfloat16 [8192, 1024], P(('rep', 'grp')), may hold values from -6 to 6
- cotangent: bfloat16 [8192, 1024], P(('rep', 'grp')), may hold values from -6 to 6
- tile_seq: int32 [64], P(('rep', 'grp')), may hold values from 0 to 63, as said below
- seq_lens: int32 [64], replicated, may hold values from 1 to 256, as said below
- attn_norm_gain: bfloat16 [1024], P('grp'), may hold values from 0.099609375 to 1.8984375
- attn_norm_bias: bfloat16 [1024], P('grp'), may hold values from -3 to 3
- qkv_weight: bfloat16 [1024, 3072], P('grp')
- query_bias: bfloat16 [1024], P('grp'), may hold values from -3 to 3
- value_bias: bfloat16 [1024], P('grp'), may hold values from -3 to 3
- out_weight: bfloat16 [1024, 1024], P('grp'), may hold values from -1 to 1
- out_bias: bfloat16 [1024], P('grp'), may hold values from -3 to 3
- ffn_norm_gain: bfloat16 [1024], P('grp'), may hold values from 0.099609375 to 1.8984375
- ffn_norm_bias: bfloat16 [1024], P('grp'), may hold values from -3 to 3
- up_weight: bfloat16 [1024, 4096], P('grp'), may hold values from -0.1875 to 0.1875
- up_bias: bfloat16 [4096], P('grp'), may hold values from -3 to 3
- down_weight: bfloat16 [4096, 1024], P('grp'), may hold values from -0.09375 to 0.09375
- down_bias: bfloat16 [1024], P('grp'), may hold values from -3 to 3
Outputs:
- attn_resid: bfloat16 [8192, 1024], P(('rep', 'grp'))
- layer_out: bfloat16 [8192, 1024], P(('rep', 'grp'))
- input_grad: float32 [8192, 1024], P(('rep', 'grp'))
- attn_norm_gain_grad: float32 [1024], P('grp')
- attn_norm_bias_grad: float32 [1024], P('grp')
- qkv_weight_grad: float32 [1024, 3072], P(('grp', 'rep'))
- query_bias_grad: float32 [1024], P('grp')
- value_bias_grad: float32 [1024], P('grp')
- out_weight_grad: float32 [1024, 1024], P(('grp', 'rep'))
- out_bias_grad: float32 [1024], P('grp')
- ffn_norm_gain_grad: float32 [1024], P('grp')
- ffn_norm_bias_grad: float32 [1024], P('grp')
- up_weight_grad: float32 [1024, 4096], P(('grp', 'rep'))
- up_bias_grad: float32 [4096], P('grp')
- down_weight_grad: float32 [4096, 1024], P(('grp', 'rep'))
- down_bias_grad: float32 [1024], P('grp')
The draws below stay inside these ranges and needn't reach their ends.
Inputs may be any that keep to these rules, and one draw needn't show every extreme that they name: `tile_seq`: the tiles of one sequence are consecutive tiles of one block, at most 2 of them, and no two blocks name the same sequence. `seq_lens`: A sequence held by k tiles is longer than (k - 1) * 128; some sequence has length 256.
All inputs are finite; a program needn't handle non-finite values.
Results may differ from the reference program's by a relative error of at most 0.011.
Values may be sent and summed in bfloat16 or wider, within the bound.
A program may use at most 256 MiB of HBM per device.

```python
import jax
import jax.numpy as jnp
from jax import lax

D = 1024
H = 16
FF = 4096
TILE = 128
TOK_DEV = 256
TILES = 2
SEQ_MAX = 256
TOKENS = 8192
NSEQ = 64
N_REP = 16
N_GRP = 2


def seq_layout(key):
    devices = NSEQ // TILES
    span_tiles = SEQ_MAX // TILE
    coins = jax.random.randint(jax.random.fold_in(key, 7), (devices, TILES), 0, 2)
    extra_len = jax.random.randint(jax.random.fold_in(key, 9), (devices, TILES), 0, TILE)
    run_length = jnp.zeros((devices,), jnp.int32)
    first_now = jnp.zeros((devices,), jnp.int32)
    first_list = []
    for tile_num in range(TILES):
        if tile_num == 0:
            start_flag = jnp.ones((devices,), jnp.int32)
        else:
            start_flag = jnp.where(run_length >= span_tiles, 1, coins[:, tile_num]).astype(jnp.int32)
            if tile_num < span_tiles:
                start_flag = start_flag.at[0].set(0)
        first_now = jnp.where(start_flag == 1, tile_num, first_now).astype(jnp.int32)
        run_length = jnp.where(start_flag == 1, 1, run_length + 1).astype(jnp.int32)
        first_list.append(first_now)
    first_tiles = jnp.stack(first_list, axis=1)
    tile_index = jnp.arange(TILES, dtype=jnp.int32)
    extent = jnp.sum((first_tiles[:, :, None] == tile_index[None, None, :]).astype(jnp.int32), axis=1)
    lengths = jnp.where(extent > 0, (extent - 1) * TILE + 1 + extra_len, 1 + extra_len).astype(jnp.int32)
    lengths = lengths.at[0, 0].set(SEQ_MAX)
    owners = jnp.arange(devices, dtype=jnp.int32)[:, None] * TILES + first_tiles
    return (owners.reshape(NSEQ).astype(jnp.int32), lengths.reshape(NSEQ).astype(jnp.int32))


def draw_tile_seq(key, part):
    return seq_layout(key)[0]


def draw_seq_lens(key, part):
    return seq_layout(key)[1]


def draw_qkv_weight(key, part):
    base = jnp.clip(jax.random.normal(jax.random.fold_in(key, 3), (D, 3 * D), jnp.float32), -6.0, 6.0) * D ** (-0.5)
    return base.astype(jnp.bfloat16)


def block_levels(key, shape, split, least, high):
    def one(position, parts):
        heights = jax.random.uniform(jax.random.fold_in(jax.random.fold_in(key, 6), position), (parts,), jnp.float32, least / len(split), high / len(split))
        return jnp.repeat(jnp.exp(heights), shape[position] // parts).reshape((-1,) + (1,) * (len(shape) - position - 1))

    factor_of = one(*split[0])
    for cut in split[1:]:
        factor_of = factor_of * one(*cut)
    return factor_of


def noise(stream_key, shape, spread, most, split=(), kind=jnp.bfloat16):
    result = jax.random.normal(stream_key, shape, jnp.float32) * spread
    if len(split) > 0:
        result = block_levels(stream_key, shape, split, -0.22, 0.18) * result
    return jnp.clip(result, min=-most, max=most).astype(kind)


def setup_inputs(seed: int = 0) -> dict:
    key_of = jax.random.split(jax.random.key(seed), 18)
    tokens = noise(key_of[0], (TOKENS, D), 1.0, 6.0, ((0, 32),))
    cotangent = noise(key_of[1], (TOKENS, D), 1.0, 6.0, ((0, 32),))
    tile_seq = draw_tile_seq(jax.random.fold_in(key_of[17], 71), 0)
    seq_lens = draw_seq_lens(jax.random.fold_in(key_of[17], 71), 0)
    attn_norm_gain = jnp.clip(1.0 + 0.18 * jax.random.normal(key_of[4], (D,), jnp.float32), 0.099609375, 1.8984375).astype(jnp.bfloat16)
    attn_norm_bias = noise(key_of[5], (D,), 0.5, 3.0, ((0, 2),))
    qkv_weight = draw_qkv_weight(jax.random.fold_in(key_of[17], 71), 0)
    query_bias = noise(key_of[7], (D,), 0.5, 3.0, ((0, 2),))
    value_bias = noise(key_of[8], (D,), 0.5, 3.0, ((0, 2),))
    out_weight = noise(key_of[9], (D, D), (D // 32) ** -0.5, 1.0, ((0, 2),))
    out_bias = noise(key_of[10], (D,), 0.5, 3.0, ((0, 2),))
    ffn_norm_gain = jnp.clip(1.0 + 0.18 * jax.random.normal(key_of[11], (D,), jnp.float32), 0.099609375, 1.8984375).astype(jnp.bfloat16)
    ffn_norm_bias = noise(key_of[12], (D,), 0.5, 3.0, ((0, 2),))
    up_weight = noise(key_of[13], (D, FF), D ** -0.5, 0.1875, ((0, 2),))
    up_bias = noise(key_of[14], (FF,), 0.5, 3.0, ((0, 2),))
    down_weight = noise(key_of[15], (FF, D), FF ** -0.5, 0.09375, ((0, 2),))
    down_bias = noise(key_of[16], (D,), 0.5, 3.0, ((0, 2),))
    return dict(tokens=tokens, cotangent=cotangent, tile_seq=tile_seq, seq_lens=seq_lens, attn_norm_gain=attn_norm_gain, attn_norm_bias=attn_norm_bias, qkv_weight=qkv_weight, query_bias=query_bias, value_bias=value_bias, out_weight=out_weight, out_bias=out_bias, ffn_norm_gain=ffn_norm_gain, ffn_norm_bias=ffn_norm_bias, up_weight=up_weight, up_bias=up_bias, down_weight=down_weight, down_bias=down_bias)


norm_eps = 1e-05
gelu_scale = 0.7978845608028654
gelu_cubic = 0.044715

def layer_norm_apply(values_in, gain, shift):
    centred = values_in - lax.optimization_barrier(jnp.mean(values_in, axis=-1, keepdims=True))
    rscale = lax.rsqrt(lax.optimization_barrier(jnp.mean(centred * centred, axis=-1, keepdims=True)) + norm_eps)
    normal_x = centred * rscale
    return (normal_x * gain + shift, normal_x, rscale)

def norm_backward_pass(grad_in, normal_x, rscale, gain):
    scaled = grad_in * gain
    grad_x = rscale * (scaled - lax.optimization_barrier(jnp.mean(scaled, axis=-1, keepdims=True)) - normal_x * lax.optimization_barrier(jnp.mean(scaled * normal_x, axis=-1, keepdims=True)))
    return (grad_x, lax.optimization_barrier(jnp.sum(grad_in * normal_x, axis=0)), lax.optimization_barrier(jnp.sum(grad_in, axis=0)))

def gelu_tanh(pre_act):
    return 0.5 * pre_act * (1.0 + jnp.tanh(gelu_scale * (pre_act + gelu_cubic * pre_act * pre_act * pre_act)))

def gelu_slope(pre_act):
    inner = jnp.tanh(gelu_scale * (pre_act + gelu_cubic * pre_act * pre_act * pre_act))
    return 0.5 * (1.0 + inner) + 0.5 * pre_act * (1.0 - inner * inner) * gelu_scale * (1.0 + 3.0 * gelu_cubic * pre_act * pre_act)

def slot_masks(tile_ids, lengths, slots):
    tiles = tile_ids.shape[0]
    per_tile = slots // tiles
    same_tile = tile_ids[:, None] == tile_ids[None, :]
    tile_pos = jnp.arange(tiles, dtype=jnp.int32)
    first_tile = lax.optimization_barrier(jnp.min(jnp.where(same_tile, tile_pos[None, :], tiles), axis=1)).astype(jnp.int32)
    seq_pos = jnp.arange(lengths.shape[0], dtype=jnp.int32)
    tile_len = lax.optimization_barrier(jnp.sum(jnp.where(tile_ids[:, None] == seq_pos[None, :], lengths[None, :], 0), axis=1)).astype(jnp.int32)
    slot_pos = jnp.arange(slots, dtype=jnp.int32)
    slot_seq = jnp.repeat(tile_ids, per_tile, total_repeat_length=slots)
    offset = slot_pos - jnp.repeat(first_tile * per_tile, per_tile, total_repeat_length=slots)
    live = offset < jnp.repeat(tile_len, per_tile, total_repeat_length=slots)
    allowed = (slot_seq[:, None] == slot_seq[None, :]) & live[:, None] & live[None, :] & (slot_pos[None, :] <= slot_pos[:, None])
    allowed = allowed | (slot_pos[:, None] == slot_pos[None, :])
    return (live, allowed)

def layer_block(block_x, block_cot, block_tiles, lengths, params):
    attention_gain_vector, attention_offset_vector, weight_qkv, bias_query, bias_value, weight_out, bias_out, feedforward_gain_vector, feedforward_offset_vector, weight_up, bias_up, weight_down, bias_down = params
    slots = block_x.shape[0]
    width = D
    heads = H
    head_dim = width // heads
    scale = head_dim ** (-0.5)
    live, allowed = slot_masks(block_tiles, lengths, slots)
    residual_input_rows = block_x.astype(jnp.float32)
    attention_normed_rows, attention_centred_scaled, attention_inverse_deviation = layer_norm_apply(residual_input_rows, attention_gain_vector.astype(jnp.float32), attention_offset_vector.astype(jnp.float32))
    attn_input = attention_normed_rows.astype(jnp.bfloat16)
    projected = jnp.dot(attn_input, weight_qkv, preferred_element_type=jnp.float32)
    queries = (projected[:, :width] + bias_query.astype(jnp.float32)).astype(jnp.bfloat16).reshape(slots, heads, head_dim)
    key_rows = projected[:, width:2 * width].astype(jnp.bfloat16).reshape(slots, heads, head_dim)
    value_rows = (projected[:, 2 * width:] + bias_value.astype(jnp.float32)).astype(jnp.bfloat16).reshape(slots, heads, head_dim)
    scores = jnp.einsum('qhd,khd->hqk', queries.astype(jnp.float32), key_rows.astype(jnp.float32)) * scale
    scores = jnp.where(allowed[None], scores, -1e+30)
    top_score = lax.optimization_barrier(jnp.max(scores, axis=-1, keepdims=True))
    log_total = top_score + jnp.log(lax.optimization_barrier(jnp.sum(jnp.exp(scores - top_score), axis=-1, keepdims=True)))
    attn_probs = jnp.where(allowed[None], jnp.exp(scores - log_total), 0.0)
    probs_low = attn_probs.astype(jnp.bfloat16)
    context = jnp.einsum('hqk,khd->qhd', probs_low.astype(jnp.float32), value_rows.astype(jnp.float32))
    context = context.reshape(slots, width).astype(jnp.bfloat16)
    middle_residual_rows = residual_input_rows + jnp.dot(context, weight_out, preferred_element_type=jnp.float32) + bias_out.astype(jnp.float32)
    feedforward_normed_rows, feedforward_centred_scaled, feedforward_inverse_deviation = layer_norm_apply(middle_residual_rows, feedforward_gain_vector.astype(jnp.float32), feedforward_offset_vector.astype(jnp.float32))
    ffn_input = feedforward_normed_rows.astype(jnp.bfloat16)
    up_sum = jnp.dot(ffn_input, weight_up, preferred_element_type=jnp.float32) + bias_up.astype(jnp.float32)
    hidden = gelu_tanh(up_sum).astype(jnp.bfloat16)
    final_resid = middle_residual_rows + jnp.dot(hidden, weight_down, preferred_element_type=jnp.float32) + bias_down.astype(jnp.float32)
    out_grad = block_cot.astype(jnp.float32) * live[:, None].astype(jnp.float32)
    out_low = out_grad.astype(jnp.bfloat16)
    grad_down_bias = lax.optimization_barrier(jnp.sum(out_grad, axis=0))
    grad_down = jnp.dot(hidden.T, out_low, preferred_element_type=jnp.float32)
    hidden_grad = jnp.dot(out_low, weight_down.T, preferred_element_type=jnp.float32)
    up_grad = hidden_grad * gelu_slope(up_sum)
    grad_up_bias = lax.optimization_barrier(jnp.sum(up_grad, axis=0))
    up_low = up_grad.astype(jnp.bfloat16)
    grad_up = jnp.dot(ffn_input.T, up_low, preferred_element_type=jnp.float32)
    normed_rows_gradient = jnp.dot(up_low, weight_up.T, preferred_element_type=jnp.float32)
    feedforward_backward_result, feedforward_gain_gradient, feedforward_offset_gradient = norm_backward_pass(normed_rows_gradient, feedforward_centred_scaled, feedforward_inverse_deviation, feedforward_gain_vector.astype(jnp.float32))
    resid_grad = out_grad + feedforward_backward_result
    grad_out_bias = lax.optimization_barrier(jnp.sum(resid_grad, axis=0))
    resid_low = resid_grad.astype(jnp.bfloat16)
    grad_out = jnp.dot(context.T, resid_low, preferred_element_type=jnp.float32)
    context_grad = jnp.dot(resid_low, weight_out.T, preferred_element_type=jnp.float32).astype(jnp.bfloat16)
    context_grad = context_grad.reshape(slots, heads, head_dim)
    value_grad = jnp.einsum('hqk,qhd->khd', probs_low.astype(jnp.float32), context_grad.astype(jnp.float32))
    prob_grad = jnp.einsum('qhd,khd->hqk', context_grad.astype(jnp.float32), value_rows.astype(jnp.float32))
    row_dot = lax.optimization_barrier(jnp.sum(attn_probs * prob_grad, axis=-1, keepdims=True))
    score_grad = (scale * attn_probs * (prob_grad - row_dot)).astype(jnp.bfloat16)
    query_grad = jnp.einsum('hqk,khd->qhd', score_grad.astype(jnp.float32), key_rows.astype(jnp.float32)).reshape(slots, width)
    key_grad = jnp.einsum('hqk,qhd->khd', score_grad.astype(jnp.float32), queries.astype(jnp.float32)).reshape(slots, width)
    value_grad = value_grad.reshape(slots, width)
    grad_query_bias = lax.optimization_barrier(jnp.sum(query_grad, axis=0))
    grad_value_bias = lax.optimization_barrier(jnp.sum(value_grad, axis=0))
    proj_grad = jnp.concatenate([query_grad, key_grad, value_grad], axis=1).astype(jnp.bfloat16)
    grad_qkv = jnp.dot(attn_input.T, proj_grad, preferred_element_type=jnp.float32)
    normed_backward_result = jnp.dot(proj_grad, weight_qkv.T, preferred_element_type=jnp.float32)
    attention_backward_result, attention_gain_gradient, attention_offset_gradient = norm_backward_pass(normed_backward_result, attention_centred_scaled, attention_inverse_deviation, attention_gain_vector.astype(jnp.float32))
    input_grad = resid_grad + attention_backward_result
    outputs = (middle_residual_rows.astype(jnp.bfloat16), final_resid.astype(jnp.bfloat16), input_grad)
    grads = (attention_gain_gradient, attention_offset_gradient, grad_qkv, grad_query_bias, grad_value_bias, grad_out, grad_out_bias, feedforward_gain_gradient, feedforward_offset_gradient, grad_up, grad_up_bias, grad_down, grad_down_bias)
    return (outputs, grads)

def reference(tokens, cotangent, tile_seq, seq_lens, attn_norm_gain, attn_norm_bias, qkv_weight, query_bias, value_bias, out_weight, out_bias, ffn_norm_gain, ffn_norm_bias, up_weight, up_bias, down_weight, down_bias):
    blocks = N_REP * N_GRP
    params = (attn_norm_gain, attn_norm_bias, qkv_weight, query_bias, value_bias, out_weight, out_bias, ffn_norm_gain, ffn_norm_bias, up_weight, up_bias, down_weight, down_bias)

    def step_block(carry, inputs):
        block_x, block_cot, block_tiles = inputs
        outputs, grads = layer_block(block_x, block_cot, block_tiles, seq_lens, params)
        return (tuple((total + grad for total, grad in zip(carry, grads))), outputs)
    start_sums = tuple((jnp.zeros(param.shape, jnp.float32) for param in params))
    inputs = (tokens.reshape(blocks, TOK_DEV, D), cotangent.reshape(blocks, TOK_DEV, D), tile_seq.reshape(blocks, TILES))
    sums, stacked = lax.scan(step_block, start_sums, inputs)
    mid_out = stacked[0].reshape(TOKENS, D)
    final_out = stacked[1].reshape(TOKENS, D)
    input_grad = stacked[2].reshape(TOKENS, D)
    return (mid_out, final_out, input_grad, sums[0], sums[1], sums[2], sums[3], sums[4], sums[5], sums[6], sums[7], sums[8], sums[9], sums[10], sums[11], sums[12])
```

```python
import jax
import jax.numpy as jnp
from jax import lax
from jax.sharding import PartitionSpec as P

H = 16


norm_eps = 1e-05
gelu_scale = 0.7978845608028654
gelu_cubic = 0.044715


def layer_norm_apply(values_in, gain, shift):
    centred = values_in - jnp.mean(values_in, axis=-1, keepdims=True)
    rscale = lax.rsqrt(jnp.mean(centred * centred, axis=-1, keepdims=True) + norm_eps)
    normal_x = centred * rscale
    return (normal_x * gain + shift, normal_x, rscale)


def norm_backward_pass(grad_in, normal_x, rscale, gain):
    scaled = grad_in * gain
    grad_x = rscale * (
        scaled
        - jnp.mean(scaled, axis=-1, keepdims=True)
        - normal_x * jnp.mean(scaled * normal_x, axis=-1, keepdims=True)
    )
    return (grad_x, jnp.sum(grad_in * normal_x, axis=0), jnp.sum(grad_in, axis=0))


def gelu_tanh(pre_act):
    return (
        0.5
        * pre_act
        * (1.0 + jnp.tanh(gelu_scale * (pre_act + gelu_cubic * pre_act * pre_act * pre_act)))
    )


def gelu_slope(pre_act):
    inner = jnp.tanh(gelu_scale * (pre_act + gelu_cubic * pre_act * pre_act * pre_act))
    return 0.5 * (1.0 + inner) + 0.5 * pre_act * (1.0 - inner * inner) * gelu_scale * (
        1.0 + 3.0 * gelu_cubic * pre_act * pre_act
    )


def slot_masks(tile_ids, lengths, slots):
    tiles = tile_ids.shape[0]
    per_tile = slots // tiles
    same_tile = tile_ids[:, None] == tile_ids[None, :]
    tile_pos = jnp.arange(tiles, dtype=jnp.int32)
    first_tile = jnp.min(jnp.where(same_tile, tile_pos[None, :], tiles), axis=1)
    seq_pos = jnp.arange(lengths.shape[0], dtype=jnp.int32)
    tile_len = jnp.sum(
        jnp.where(tile_ids[:, None] == seq_pos[None, :], lengths[None, :], 0), axis=1
    )
    slot_pos = jnp.arange(slots, dtype=jnp.int32)
    slot_seq = jnp.repeat(tile_ids, per_tile, total_repeat_length=slots)
    offset = slot_pos - jnp.repeat(first_tile * per_tile, per_tile, total_repeat_length=slots)
    live = offset < jnp.repeat(tile_len, per_tile, total_repeat_length=slots)
    allowed = (
        (slot_seq[:, None] == slot_seq[None, :])
        & live[:, None]
        & live[None, :]
        & (slot_pos[None, :] <= slot_pos[:, None])
    )
    allowed = allowed | (slot_pos[:, None] == slot_pos[None, :])
    return (live, allowed)


def outer_sum(left, right):
    return lax.dot_general(
        left, right, (((0,), (0,)), ((), ())), preferred_element_type=jnp.float32
    )


def times_transpose(left, right):
    return lax.dot_general(
        left, right, (((1,), (1,)), ((), ())), preferred_element_type=jnp.float32
    )


def swap(values, bit):
    if bit == "g":
        return lax.ppermute(values, "grp", [(0, 1), (1, 0)])
    count = lax.axis_size("rep")
    return lax.ppermute(values, "rep", [(i, i ^ (1 << bit)) for i in range(count)])


def my_bit(bit):
    if bit == "g":
        return lax.axis_index("grp")
    return (lax.axis_index("rep") >> bit) & 1


def gather_rows(shard, bits):
    rows, cols = shard.shape
    count = 1 << len(bits)
    size = rows // count
    place = sum(my_bit(b) << k for k, b in enumerate(bits))
    own = lax.dynamic_slice_in_dim(shard, place * size, size, 0)
    pieces = [(0, swap(own, "g"))]
    for k, b in enumerate(bits):
        pieces = pieces + [(rel ^ (1 << k), swap(p, b)) for rel, p in pieces]
    whole = jnp.concatenate([shard, shard], axis=0)
    base = (1 - lax.axis_index("grp")) * rows
    for rel, p in pieces:
        whole = lax.dynamic_update_slice_in_dim(whole, p, base + (place ^ rel) * size, 0)
    return whole


def scatter_rows(grad, order):
    rep_bits = lax.axis_size("rep").bit_length() - 1
    left = ["g"] + list(range(rep_bits - 1, -1, -1))
    cols = grad.shape[1]
    part = grad.astype(jnp.bfloat16)
    order = [b for b in order if b in left] + [b for b in left if b not in order]
    for step, b in enumerate(order):
        at = left.index(b)
        rows = part.shape[0]
        view = part.reshape(1 << at, 2, rows >> (at + 1), cols)
        bit = my_bit(b)
        send = lax.dynamic_index_in_dim(view, 1 - bit, 1, False).reshape(rows // 2, cols)
        keep = lax.dynamic_index_in_dim(view, bit, 1, False).reshape(rows // 2, cols)
        part = keep.astype(jnp.float32) + swap(send, b).astype(jnp.float32)
        if step + 1 < len(order):
            part = part.astype(jnp.bfloat16)
        left.remove(b)
    return part


def scatter_columns(grad, orders):
    width = grad.shape[1] // len(orders)
    return jnp.concatenate(
        [scatter_rows(grad[:, i * width : (i + 1) * width], o) for i, o in enumerate(orders)],
        axis=1,
    )


def gather_vectors(shards_in):
    packed = jnp.concatenate(shards_in)
    other = swap(packed, "g")
    first = lax.axis_index("grp") == 0
    low, high = jnp.where(first, packed, other), jnp.where(first, other, packed)
    out, at = [], 0
    for v in shards_in:
        n = v.shape[0]
        out.append(jnp.concatenate([low[at : at + n], high[at : at + n]]))
        at += n
    return out


def sum_vectors(vectors):
    halves = [v.reshape(2, -1) for v in vectors]
    packed = jnp.concatenate(halves, axis=1)
    lanes = 128
    packed = packed.reshape(2, -1, lanes)
    mine = lax.axis_index("grp")
    total = lax.dynamic_index_in_dim(packed, mine, 0, False) + swap(
        lax.dynamic_index_in_dim(packed, 1 - mine, 0, False), "g"
    )
    for bit in range(lax.axis_size("rep").bit_length() - 1):
        total = total + swap(total, bit)
    total = total.reshape(-1)
    out, at = [], 0
    for h in halves:
        out.append(total[at : at + h.shape[1]])
        at += h.shape[1]
    return out


def shards(
    tokens,
    cotangent,
    tile_seq,
    seq_lens,
    attn_norm_gain,
    attn_norm_bias,
    qkv_weight,
    query_bias,
    value_bias,
    out_weight,
    out_bias,
    ffn_norm_gain,
    ffn_norm_bias,
    up_weight,
    up_bias,
    down_weight,
    down_bias,
):
    (
        attention_gain_vector,
        attention_offset_vector,
        bias_query,
        bias_value,
        bias_out,
        feedforward_gain_vector,
        feedforward_offset_vector,
        bias_up,
        bias_down,
    ) = gather_vectors(
        [
            attn_norm_gain,
            attn_norm_bias,
            query_bias,
            value_bias,
            out_bias,
            ffn_norm_gain,
            ffn_norm_bias,
            up_bias,
            down_bias,
        ]
    )
    weight_qkv = gather_rows(qkv_weight, (1, 0))
    weight_out = gather_rows(out_weight, (2, 0))
    weight_up = gather_rows(up_weight, (2, 1, 0))
    weight_down = gather_rows(down_weight, (1, 2, 0))
    slots, width = tokens.shape
    heads = H
    head_dim = width // heads
    scale = head_dim ** (-0.5)
    live, allowed = slot_masks(tile_seq, seq_lens, slots)
    residual_input_rows = tokens.astype(jnp.float32)
    attention_normed_rows, attention_centred_scaled, attention_inverse_deviation = layer_norm_apply(
        residual_input_rows,
        attention_gain_vector.astype(jnp.float32),
        attention_offset_vector.astype(jnp.float32),
    )
    attn_input = attention_normed_rows.astype(jnp.bfloat16)
    projected = jnp.dot(attn_input, weight_qkv, preferred_element_type=jnp.float32)
    queries = (
        (projected[:, :width] + bias_query.astype(jnp.float32))
        .astype(jnp.bfloat16)
        .reshape(slots, heads, head_dim)
    )
    key_rows = projected[:, width : 2 * width].astype(jnp.bfloat16).reshape(slots, heads, head_dim)
    value_rows = (
        (projected[:, 2 * width :] + bias_value.astype(jnp.float32))
        .astype(jnp.bfloat16)
        .reshape(slots, heads, head_dim)
    )
    scores = (
        jnp.einsum("qhd,khd->hqk", queries, key_rows, preferred_element_type=jnp.float32) * scale
    )
    scores = jnp.where(allowed[None], scores, -1e30)
    top_score = jnp.max(scores, axis=-1, keepdims=True)
    log_total = top_score + jnp.log(jnp.sum(jnp.exp(scores - top_score), axis=-1, keepdims=True))
    probs_low = jnp.where(allowed[None], jnp.exp(scores - log_total), 0.0).astype(jnp.bfloat16)
    context = jnp.einsum("hqk,khd->qhd", probs_low, value_rows, preferred_element_type=jnp.float32)
    context = context.reshape(slots, width).astype(jnp.bfloat16)
    middle_residual_rows = (
        residual_input_rows
        + jnp.dot(context, weight_out, preferred_element_type=jnp.float32)
        + bias_out.astype(jnp.float32)
    )
    feedforward_normed_rows, feedforward_centred_scaled, feedforward_inverse_deviation = (
        layer_norm_apply(
            middle_residual_rows,
            feedforward_gain_vector.astype(jnp.float32),
            feedforward_offset_vector.astype(jnp.float32),
        )
    )
    ffn_input = feedforward_normed_rows.astype(jnp.bfloat16)
    up_sum = jnp.dot(ffn_input, weight_up, preferred_element_type=jnp.float32) + bias_up.astype(
        jnp.float32
    )
    hidden = gelu_tanh(up_sum).astype(jnp.bfloat16)
    ffn_out = jnp.dot(hidden, weight_down, preferred_element_type=jnp.float32)
    final_resid = middle_residual_rows + ffn_out + bias_down.astype(jnp.float32)
    out_grad = cotangent.astype(jnp.float32) * live[:, None].astype(jnp.float32)
    out_low = out_grad.astype(jnp.bfloat16)
    grad_down_bias = jnp.sum(out_grad, axis=0)
    grad_down = outer_sum(hidden, out_low)
    hidden_grad = times_transpose(out_low, weight_down)
    up_grad = hidden_grad * gelu_slope(up_sum)
    grad_up_bias = jnp.sum(up_grad, axis=0)
    up_low = up_grad.astype(jnp.bfloat16)
    grad_up = outer_sum(ffn_input, up_low)
    normed_rows_gradient = times_transpose(up_low, weight_up)
    grad_down = scatter_columns(grad_down, ((0, "g", 1, 2, 3), (0, 1, 2, "g", 3)))
    grad_up = scatter_columns(grad_up, ((0, 2, "g", 1, 3), (0, "g", 2, 1, 3)))
    feedforward_backward_result, feedforward_gain_gradient, feedforward_offset_gradient = (
        norm_backward_pass(
            normed_rows_gradient,
            feedforward_centred_scaled,
            feedforward_inverse_deviation,
            feedforward_gain_vector.astype(jnp.float32),
        )
    )
    resid_grad = out_grad + feedforward_backward_result
    grad_out_bias = jnp.sum(resid_grad, axis=0)
    resid_low = resid_grad.astype(jnp.bfloat16)
    grad_out = outer_sum(context, resid_low)
    context_grad = (
        times_transpose(resid_low, weight_out).astype(jnp.bfloat16).reshape(slots, heads, head_dim)
    )
    again_scores = (
        jnp.einsum("qhd,khd->hqk", queries, key_rows, preferred_element_type=jnp.float32) * scale
    )
    attn_probs = jnp.where(
        allowed[None], jnp.exp(jnp.where(allowed[None], again_scores, -1e30) - log_total), 0.0
    )
    again_low = attn_probs.astype(jnp.bfloat16)
    value_grad = jnp.einsum(
        "hqk,qhd->khd", again_low, context_grad, preferred_element_type=jnp.float32
    )
    prob_grad = jnp.einsum(
        "qhd,khd->hqk", context_grad, value_rows, preferred_element_type=jnp.float32
    )
    row_dot = jnp.sum(attn_probs * prob_grad, axis=-1, keepdims=True)
    score_grad = (scale * attn_probs * (prob_grad - row_dot)).astype(jnp.bfloat16)
    query_grad = jnp.einsum(
        "hqk,khd->qhd", score_grad, key_rows, preferred_element_type=jnp.float32
    ).reshape(slots, width)
    key_grad = jnp.einsum(
        "hqk,qhd->khd", score_grad, queries, preferred_element_type=jnp.float32
    ).reshape(slots, width)
    value_grad = value_grad.reshape(slots, width)
    grad_query_bias = jnp.sum(query_grad, axis=0)
    grad_value_bias = jnp.sum(value_grad, axis=0)
    proj_grad = jnp.concatenate([query_grad, key_grad, value_grad], axis=1).astype(jnp.bfloat16)
    grad_qkv = outer_sum(attn_input, proj_grad)
    normed_backward_result = times_transpose(proj_grad, weight_qkv)
    attention_backward_result, attention_gain_gradient, attention_offset_gradient = (
        norm_backward_pass(
            normed_backward_result,
            attention_centred_scaled,
            attention_inverse_deviation,
            attention_gain_vector.astype(jnp.float32),
        )
    )
    input_grad = resid_grad + attention_backward_result
    grad_out = scatter_rows(grad_out, (0, 1, 2, "g", 3))
    grad_qkv = scatter_columns(
        grad_qkv, ((0, "g", 1, 2, 3), (0, 1, 2, "g", 3), (0, 2, "g", 1, 3))
    )
    (
        attention_gain_gradient,
        attention_offset_gradient,
        grad_query_bias,
        grad_value_bias,
        grad_out_bias,
        feedforward_gain_gradient,
        feedforward_offset_gradient,
        grad_up_bias,
        grad_down_bias,
    ) = sum_vectors(
        [
            attention_gain_gradient,
            attention_offset_gradient,
            grad_query_bias,
            grad_value_bias,
            grad_out_bias,
            feedforward_gain_gradient,
            feedforward_offset_gradient,
            grad_up_bias,
            grad_down_bias,
        ]
    )
    return (
        middle_residual_rows.astype(jnp.bfloat16),
        final_resid.astype(jnp.bfloat16),
        input_grad,
        attention_gain_gradient,
        attention_offset_gradient,
        grad_qkv,
        grad_query_bias,
        grad_value_bias,
        grad_out,
        grad_out_bias,
        feedforward_gain_gradient,
        feedforward_offset_gradient,
        grad_up,
        grad_up_bias,
        grad_down,
        grad_down_bias,
    )


def solution(mesh):
    return jax.shard_map(
        shards,
        mesh=mesh,
        in_specs=(
            P(("rep", "grp"), None),
            P(("rep", "grp"), None),
            P(("rep", "grp")),
            P(),
            P("grp"),
            P("grp"),
            P("grp", None),
            P("grp"),
            P("grp"),
            P("grp", None),
            P("grp"),
            P("grp"),
            P("grp"),
            P("grp", None),
            P("grp"),
            P("grp", None),
            P("grp"),
        ),
        out_specs=(
            P(("rep", "grp"), None),
            P(("rep", "grp"), None),
            P(("rep", "grp"), None),
            P("grp"),
            P("grp"),
            P(("grp", "rep"), None),
            P("grp"),
            P("grp"),
            P(("grp", "rep"), None),
            P("grp"),
            P("grp"),
            P("grp"),
            P(("grp", "rep"), None),
            P("grp"),
            P(("grp", "rep"), None),
            P("grp"),
        ),
        check_vma=False,
    )
```

```python
import jax
import jax.numpy as jnp
from jax import lax
from jax.sharding import PartitionSpec as P

H = 16


norm_eps = 1e-05
gelu_scale = 0.7978845608028654
gelu_cubic = 0.044715


def layer_norm_apply(values_in, gain, shift):
    centred = values_in - jnp.mean(values_in, axis=-1, keepdims=True)
    rscale = lax.rsqrt(jnp.mean(centred * centred, axis=-1, keepdims=True) + norm_eps)
    normal_x = centred * rscale
    return (normal_x * gain + shift, normal_x, rscale)


def norm_backward_pass(grad_in, normal_x, rscale, gain):
    scaled = grad_in * gain
    grad_x = rscale * (
        scaled
        - jnp.mean(scaled, axis=-1, keepdims=True)
        - normal_x * jnp.mean(scaled * normal_x, axis=-1, keepdims=True)
    )
    return (grad_x, jnp.sum(grad_in * normal_x, axis=0), jnp.sum(grad_in, axis=0))


def gelu_tanh(pre_act):
    return (
        0.5
        * pre_act
        * (1.0 + jnp.tanh(gelu_scale * (pre_act + gelu_cubic * pre_act * pre_act * pre_act)))
    )


def gelu_slope(pre_act):
    inner = jnp.tanh(gelu_scale * (pre_act + gelu_cubic * pre_act * pre_act * pre_act))
    return 0.5 * (1.0 + inner) + 0.5 * pre_act * (1.0 - inner * inner) * gelu_scale * (
        1.0 + 3.0 * gelu_cubic * pre_act * pre_act
    )


def slot_masks(tile_ids, lengths, slots):
    tiles = tile_ids.shape[0]
    per_tile = slots // tiles
    same_tile = tile_ids[:, None] == tile_ids[None, :]
    tile_pos = jnp.arange(tiles, dtype=jnp.int32)
    first_tile = jnp.min(jnp.where(same_tile, tile_pos[None, :], tiles), axis=1)
    seq_pos = jnp.arange(lengths.shape[0], dtype=jnp.int32)
    tile_len = jnp.sum(
        jnp.where(tile_ids[:, None] == seq_pos[None, :], lengths[None, :], 0), axis=1
    )
    slot_pos = jnp.arange(slots, dtype=jnp.int32)
    slot_seq = jnp.repeat(tile_ids, per_tile, total_repeat_length=slots)
    offset = slot_pos - jnp.repeat(first_tile * per_tile, per_tile, total_repeat_length=slots)
    live = offset < jnp.repeat(tile_len, per_tile, total_repeat_length=slots)
    allowed = (
        (slot_seq[:, None] == slot_seq[None, :])
        & live[:, None]
        & live[None, :]
        & (slot_pos[None, :] <= slot_pos[:, None])
    )
    allowed = allowed | (slot_pos[:, None] == slot_pos[None, :])
    return (live, allowed)


def outer_sum(left, right):
    return lax.dot_general(
        left, right, (((0,), (0,)), ((), ())), preferred_element_type=jnp.float32
    )


def times_transpose(left, right):
    return lax.dot_general(
        left, right, (((1,), (1,)), ((), ())), preferred_element_type=jnp.float32
    )


def swap(values, bit):
    if bit == "g":
        return lax.ppermute(values, "grp", [(0, 1), (1, 0)])
    count = lax.axis_size("rep")
    return lax.ppermute(values, "rep", [(i, i ^ (1 << bit)) for i in range(count)])


def my_bit(bit):
    if bit == "g":
        return lax.axis_index("grp")
    return (lax.axis_index("rep") >> bit) & 1


def piece_place(bits):
    return sum(my_bit(b) << k for k, b in enumerate(bits))


def own_piece(shard, bits):
    size = shard.shape[0] >> len(bits)
    return lax.dynamic_slice_in_dim(shard, piece_place(bits) * size, size, 0)


def spread_pieces(piece, bits):
    pieces = [piece]
    for b in bits:
        pieces = pieces + [swap(p, b) for p in pieces]
    return pieces


def join_rows(shard, pieces, bits):
    rows = shard.shape[0]
    size = rows >> len(bits)
    place = piece_place(bits)
    whole = jnp.concatenate([shard, shard], axis=0)
    base = (1 - lax.axis_index("grp")) * rows
    for rel, p in enumerate(pieces):
        whole = lax.dynamic_update_slice_in_dim(whole, p, base + (place ^ rel) * size, 0)
    return whole


def all_bits():
    return ["g"] + list(range(lax.axis_size("rep").bit_length() - 2, -1, -1))


def split_half(part, left, b):
    at = left.index(b)
    rows, cols = part.shape
    view = part.reshape(1 << at, 2, rows >> (at + 1), cols)
    bit = my_bit(b)
    keep = lax.dynamic_index_in_dim(view, bit, 1, False).reshape(rows // 2, cols)
    send = lax.dynamic_index_in_dim(view, 1 - bit, 1, False).reshape(rows // 2, cols)
    return keep, send


def core_halves(grad):
    return split_half(grad.astype(jnp.bfloat16), all_bits(), 0)


def join_half(keep, received):
    return keep.astype(jnp.float32) + received.astype(jnp.float32)


def scatter_rest(grad, orders):
    width = grad.shape[1] // len(orders)
    done = []
    for i, order in enumerate(orders):
        left = [b for b in all_bits() if b != 0]
        order = [b for b in order if b in left] + [b for b in left if b not in order]
        part = grad[:, i * width : (i + 1) * width]
        for b in order:
            keep, send = split_half(part.astype(jnp.bfloat16), left, b)
            part = join_half(keep, swap(send, b))
            left.remove(b)
        done.append(part)
    return jnp.concatenate(done, axis=1)


def gather_vectors(shards_in):
    packed = jnp.concatenate(shards_in)
    other = swap(packed, "g")
    first = lax.axis_index("grp") == 0
    low, high = jnp.where(first, packed, other), jnp.where(first, other, packed)
    out, at = [], 0
    for v in shards_in:
        n = v.shape[0]
        out.append(jnp.concatenate([low[at : at + n], high[at : at + n]]))
        at += n
    return out


def sum_vectors(vectors):
    halves = [v.reshape(2, -1) for v in vectors]
    packed = jnp.concatenate(halves, axis=1)
    lanes = 128
    packed = packed.reshape(2, -1, lanes)
    mine = lax.axis_index("grp")
    total = lax.dynamic_index_in_dim(packed, mine, 0, False) + swap(
        lax.dynamic_index_in_dim(packed, 1 - mine, 0, False), "g"
    )
    for bit in range(lax.axis_size("rep").bit_length() - 1):
        total = total + swap(total, bit)
    total = total.reshape(-1)
    out, at = [], 0
    for h in halves:
        out.append(total[at : at + h.shape[1]])
        at += h.shape[1]
    return out


def shards(
    tokens,
    cotangent,
    tile_seq,
    seq_lens,
    attn_norm_gain,
    attn_norm_bias,
    qkv_weight,
    query_bias,
    value_bias,
    out_weight,
    out_bias,
    ffn_norm_gain,
    ffn_norm_bias,
    up_weight,
    up_bias,
    down_weight,
    down_bias,
):
    (
        attention_gain_vector,
        attention_offset_vector,
        bias_query,
        bias_value,
        bias_out,
        feedforward_gain_vector,
        feedforward_offset_vector,
        bias_up,
        bias_down,
    ) = gather_vectors(
        [
            attn_norm_gain,
            attn_norm_bias,
            query_bias,
            value_bias,
            out_bias,
            ffn_norm_gain,
            ffn_norm_bias,
            up_bias,
            down_bias,
        ]
    )
    qkv_bits, out_bits, up_bits, down_bits = (1, 0), (2, 0), (2, 1, 0), (1, 2, 0)
    piece_qkv = swap(own_piece(qkv_weight, qkv_bits), "g")
    piece_out, piece_up, piece_down, piece_qkv = lax.optimization_barrier(
        (
            own_piece(out_weight, out_bits),
            own_piece(up_weight, up_bits),
            own_piece(down_weight, down_bits),
            piece_qkv,
        )
    )
    pieces_qkv = spread_pieces(piece_qkv, qkv_bits)
    weight_qkv = join_rows(qkv_weight, pieces_qkv, qkv_bits)
    pieces_out = spread_pieces(swap(piece_out, "g"), out_bits)
    pieces_up = spread_pieces(swap(piece_up, "g"), up_bits)
    pieces_down = spread_pieces(swap(piece_down, "g"), down_bits)
    slots, width = tokens.shape
    heads = H
    head_dim = width // heads
    scale = head_dim ** (-0.5)
    live, allowed = slot_masks(tile_seq, seq_lens, slots)
    residual_input_rows = tokens.astype(jnp.float32)
    attention_normed_rows, attention_centred_scaled, attention_inverse_deviation = layer_norm_apply(
        residual_input_rows,
        attention_gain_vector.astype(jnp.float32),
        attention_offset_vector.astype(jnp.float32),
    )
    attn_input = attention_normed_rows.astype(jnp.bfloat16)
    projected = jnp.dot(attn_input, weight_qkv, preferred_element_type=jnp.float32)
    queries = (
        (projected[:, :width] + bias_query.astype(jnp.float32))
        .astype(jnp.bfloat16)
        .reshape(slots, heads, head_dim)
    )
    key_rows = projected[:, width : 2 * width].astype(jnp.bfloat16).reshape(slots, heads, head_dim)
    value_rows = (
        (projected[:, 2 * width :] + bias_value.astype(jnp.float32))
        .astype(jnp.bfloat16)
        .reshape(slots, heads, head_dim)
    )
    scores = (
        jnp.einsum("qhd,khd->hqk", queries, key_rows, preferred_element_type=jnp.float32) * scale
    )
    scores = jnp.where(allowed[None], scores, -1e30)
    top_score = jnp.max(scores, axis=-1, keepdims=True)
    log_total = top_score + jnp.log(jnp.sum(jnp.exp(scores - top_score), axis=-1, keepdims=True))
    probs_low = jnp.where(allowed[None], jnp.exp(scores - log_total), 0.0).astype(jnp.bfloat16)
    context = jnp.einsum("hqk,khd->qhd", probs_low, value_rows, preferred_element_type=jnp.float32)
    context = context.reshape(slots, width).astype(jnp.bfloat16)
    context, pieces_out = lax.optimization_barrier((context, pieces_out))
    weight_out = join_rows(out_weight, pieces_out, out_bits)
    middle_residual_rows = (
        residual_input_rows
        + jnp.dot(context, weight_out, preferred_element_type=jnp.float32)
        + bias_out.astype(jnp.float32)
    )
    feedforward_normed_rows, feedforward_centred_scaled, feedforward_inverse_deviation = (
        layer_norm_apply(
            middle_residual_rows,
            feedforward_gain_vector.astype(jnp.float32),
            feedforward_offset_vector.astype(jnp.float32),
        )
    )
    ffn_input = feedforward_normed_rows.astype(jnp.bfloat16)
    ffn_input, pieces_up = lax.optimization_barrier((ffn_input, pieces_up))
    weight_up = join_rows(up_weight, pieces_up, up_bits)
    up_sum = jnp.dot(ffn_input, weight_up, preferred_element_type=jnp.float32) + bias_up.astype(
        jnp.float32
    )
    hidden = gelu_tanh(up_sum).astype(jnp.bfloat16)
    hidden, pieces_down = lax.optimization_barrier((hidden, pieces_down))
    weight_down = join_rows(down_weight, pieces_down, down_bits)
    ffn_out = jnp.dot(hidden, weight_down, preferred_element_type=jnp.float32)
    final_resid = middle_residual_rows + ffn_out + bias_down.astype(jnp.float32)
    out_grad = cotangent.astype(jnp.float32) * live[:, None].astype(jnp.float32)
    out_low = out_grad.astype(jnp.bfloat16)
    grad_down_bias = jnp.sum(out_grad, axis=0)
    grad_down = outer_sum(hidden, out_low)
    hidden_grad = times_transpose(out_low, weight_down)
    up_grad = hidden_grad * gelu_slope(up_sum)
    grad_up_bias = jnp.sum(up_grad, axis=0)
    up_low = up_grad.astype(jnp.bfloat16)
    grad_up = outer_sum(ffn_input, up_low)
    normed_rows_gradient = times_transpose(up_low, weight_up)
    keep_down, send_down = core_halves(grad_down)
    keep_up, send_up = core_halves(grad_up)
    normed_rows_gradient, send_down, send_up = lax.optimization_barrier(
        (normed_rows_gradient, send_down, send_up)
    )
    recv_down, recv_up = swap(send_down, 0), swap(send_up, 0)
    feedforward_backward_result, feedforward_gain_gradient, feedforward_offset_gradient = (
        norm_backward_pass(
            normed_rows_gradient,
            feedforward_centred_scaled,
            feedforward_inverse_deviation,
            feedforward_gain_vector.astype(jnp.float32),
        )
    )
    resid_grad = out_grad + feedforward_backward_result
    grad_out_bias = jnp.sum(resid_grad, axis=0)
    resid_low = resid_grad.astype(jnp.bfloat16)
    grad_out = outer_sum(context, resid_low)
    context_grad = (
        times_transpose(resid_low, weight_out).astype(jnp.bfloat16).reshape(slots, heads, head_dim)
    )
    again_scores = (
        jnp.einsum("qhd,khd->hqk", queries, key_rows, preferred_element_type=jnp.float32) * scale
    )
    attn_probs = jnp.where(
        allowed[None], jnp.exp(jnp.where(allowed[None], again_scores, -1e30) - log_total), 0.0
    )
    again_low = attn_probs.astype(jnp.bfloat16)
    half_down = join_half(keep_down, recv_down).astype(jnp.bfloat16)
    half_up = join_half(keep_up, recv_up).astype(jnp.bfloat16)
    context_grad, half_down, half_up = lax.optimization_barrier((context_grad, half_down, half_up))
    grad_down = scatter_rest(half_down, (("g", 1, 2, 3), (1, 2, "g", 3)))
    grad_up = scatter_rest(half_up, ((2, "g", 1, 3), ("g", 2, 1, 3)))
    value_grad = jnp.einsum(
        "hqk,qhd->khd", again_low, context_grad, preferred_element_type=jnp.float32
    )
    prob_grad = jnp.einsum(
        "qhd,khd->hqk", context_grad, value_rows, preferred_element_type=jnp.float32
    )
    row_dot = jnp.sum(attn_probs * prob_grad, axis=-1, keepdims=True)
    score_grad = (scale * attn_probs * (prob_grad - row_dot)).astype(jnp.bfloat16)
    query_grad = jnp.einsum(
        "hqk,khd->qhd", score_grad, key_rows, preferred_element_type=jnp.float32
    ).reshape(slots, width)
    key_grad = jnp.einsum(
        "hqk,qhd->khd", score_grad, queries, preferred_element_type=jnp.float32
    ).reshape(slots, width)
    value_grad = value_grad.reshape(slots, width)
    grad_query_bias = jnp.sum(query_grad, axis=0)
    grad_value_bias = jnp.sum(value_grad, axis=0)
    proj_grad = jnp.concatenate([query_grad, key_grad, value_grad], axis=1).astype(jnp.bfloat16)
    grad_qkv = outer_sum(attn_input, proj_grad)
    normed_backward_result = times_transpose(proj_grad, weight_qkv)
    attention_backward_result, attention_gain_gradient, attention_offset_gradient = (
        norm_backward_pass(
            normed_backward_result,
            attention_centred_scaled,
            attention_inverse_deviation,
            attention_gain_vector.astype(jnp.float32),
        )
    )
    input_grad = resid_grad + attention_backward_result
    keep_out, send_out = core_halves(grad_out)
    grad_out = scatter_rest(join_half(keep_out, swap(send_out, 0)), ((1, 2, "g", 3),))
    keep_qkv, send_qkv = core_halves(grad_qkv)
    grad_qkv = scatter_rest(
        join_half(keep_qkv, swap(send_qkv, 0)),
        (("g", 1, 2, 3), (1, 2, "g", 3), (2, "g", 1, 3)),
    )
    (
        attention_gain_gradient,
        attention_offset_gradient,
        grad_query_bias,
        grad_value_bias,
        grad_out_bias,
        feedforward_gain_gradient,
        feedforward_offset_gradient,
        grad_up_bias,
        grad_down_bias,
    ) = sum_vectors(
        [
            attention_gain_gradient,
            attention_offset_gradient,
            grad_query_bias,
            grad_value_bias,
            grad_out_bias,
            feedforward_gain_gradient,
            feedforward_offset_gradient,
            grad_up_bias,
            grad_down_bias,
        ]
    )
    return (
        middle_residual_rows.astype(jnp.bfloat16),
        final_resid.astype(jnp.bfloat16),
        input_grad,
        attention_gain_gradient,
        attention_offset_gradient,
        grad_qkv,
        grad_query_bias,
        grad_value_bias,
        grad_out,
        grad_out_bias,
        feedforward_gain_gradient,
        feedforward_offset_gradient,
        grad_up,
        grad_up_bias,
        grad_down,
        grad_down_bias,
    )


def solution(mesh):
    return jax.shard_map(
        shards,
        mesh=mesh,
        in_specs=(
            P(("rep", "grp"), None),
            P(("rep", "grp"), None),
            P(("rep", "grp")),
            P(),
            P("grp"),
            P("grp"),
            P("grp", None),
            P("grp"),
            P("grp"),
            P("grp", None),
            P("grp"),
            P("grp"),
            P("grp"),
            P("grp", None),
            P("grp"),
            P("grp", None),
            P("grp"),
        ),
        out_specs=(
            P(("rep", "grp"), None),
            P(("rep", "grp"), None),
            P(("rep", "grp"), None),
            P("grp"),
            P("grp"),
            P(("grp", "rep"), None),
            P("grp"),
            P("grp"),
            P(("grp", "rep"), None),
            P("grp"),
            P("grp"),
            P("grp"),
            P(("grp", "rep"), None),
            P("grp"),
            P(("grp", "rep"), None),
            P("grp"),
        ),
        check_vma=False,
    )
```

```python
import jax
import jax.numpy as jnp
from jax import lax
from jax.sharding import PartitionSpec as P

H = 16


norm_eps = 1e-05
gelu_scale = 0.7978845608028654
gelu_cubic = 0.044715


def layer_norm_apply(values_in, gain, shift):
    centred = values_in - jnp.mean(values_in, axis=-1, keepdims=True)
    rscale = lax.rsqrt(jnp.mean(centred * centred, axis=-1, keepdims=True) + norm_eps)
    normal_x = centred * rscale
    return (normal_x * gain + shift, normal_x, rscale)


def norm_backward_pass(grad_in, normal_x, rscale, gain):
    scaled = grad_in * gain
    grad_x = rscale * (
        scaled
        - jnp.mean(scaled, axis=-1, keepdims=True)
        - normal_x * jnp.mean(scaled * normal_x, axis=-1, keepdims=True)
    )
    return (grad_x, jnp.sum(grad_in * normal_x, axis=0), jnp.sum(grad_in, axis=0))


def gelu_tanh(pre_act):
    return (
        0.5
        * pre_act
        * (1.0 + jnp.tanh(gelu_scale * (pre_act + gelu_cubic * pre_act * pre_act * pre_act)))
    )


def gelu_slope(pre_act):
    inner = jnp.tanh(gelu_scale * (pre_act + gelu_cubic * pre_act * pre_act * pre_act))
    return 0.5 * (1.0 + inner) + 0.5 * pre_act * (1.0 - inner * inner) * gelu_scale * (
        1.0 + 3.0 * gelu_cubic * pre_act * pre_act
    )


def slot_masks(tile_ids, lengths, slots):
    tiles = tile_ids.shape[0]
    per_tile = slots // tiles
    same_tile = tile_ids[:, None] == tile_ids[None, :]
    tile_pos = jnp.arange(tiles, dtype=jnp.int32)
    first_tile = jnp.min(jnp.where(same_tile, tile_pos[None, :], tiles), axis=1)
    seq_pos = jnp.arange(lengths.shape[0], dtype=jnp.int32)
    tile_len = jnp.sum(
        jnp.where(tile_ids[:, None] == seq_pos[None, :], lengths[None, :], 0), axis=1
    )
    slot_pos = jnp.arange(slots, dtype=jnp.int32)
    slot_seq = jnp.repeat(tile_ids, per_tile, total_repeat_length=slots)
    offset = slot_pos - jnp.repeat(first_tile * per_tile, per_tile, total_repeat_length=slots)
    live = offset < jnp.repeat(tile_len, per_tile, total_repeat_length=slots)
    allowed = (
        (slot_seq[:, None] == slot_seq[None, :])
        & live[:, None]
        & live[None, :]
        & (slot_pos[None, :] <= slot_pos[:, None])
    )
    allowed = allowed | (slot_pos[:, None] == slot_pos[None, :])
    return (live, allowed)


def outer_sum(left, right):
    return lax.dot_general(
        left, right, (((0,), (0,)), ((), ())), preferred_element_type=jnp.float32
    )


def times_transpose(left, right):
    return lax.dot_general(
        left, right, (((1,), (1,)), ((), ())), preferred_element_type=jnp.float32
    )


def swap(values, bit):
    if bit == "g":
        return lax.ppermute(values, "grp", [(0, 1), (1, 0)])
    count = lax.axis_size("rep")
    return lax.ppermute(values, "rep", [(i, i ^ (1 << bit)) for i in range(count)])


def my_bit(bit):
    if bit == "g":
        return lax.axis_index("grp")
    return (lax.axis_index("rep") >> bit) & 1


def piece_place(bits):
    return sum(my_bit(b) << k for k, b in enumerate(bits))


def own_piece(shard, bits):
    size = shard.shape[0] >> len(bits)
    return lax.dynamic_slice_in_dim(shard, piece_place(bits) * size, size, 0)


def spread_pieces(piece, bits):
    pieces = [piece]
    for b in bits:
        pieces = pieces + [swap(p, b) for p in pieces]
    return pieces


def join_rows(shard, pieces, bits):
    rows = shard.shape[0]
    size = rows >> len(bits)
    place = piece_place(bits)
    whole = jnp.concatenate([shard, shard], axis=0)
    base = (1 - lax.axis_index("grp")) * rows
    for rel, p in enumerate(pieces):
        whole = lax.dynamic_update_slice_in_dim(whole, p, base + (place ^ rel) * size, 0)
    return whole


def all_bits():
    return ["g"] + list(range(lax.axis_size("rep").bit_length() - 2, -1, -1))


def split_half(part, left, b):
    at = left.index(b)
    rows, cols = part.shape
    view = part.reshape(1 << at, 2, rows >> (at + 1), cols)
    bit = my_bit(b)
    keep = lax.dynamic_index_in_dim(view, bit, 1, False).reshape(rows // 2, cols)
    send = lax.dynamic_index_in_dim(view, 1 - bit, 1, False).reshape(rows // 2, cols)
    return keep, send


def core_halves(grad):
    return split_half(grad.astype(jnp.bfloat16), all_bits(), 0)


def join_half(keep, received):
    return keep.astype(jnp.float32) + received.astype(jnp.float32)


def halving_step(part, left, b):
    keep, send = split_half(part.astype(jnp.bfloat16), left, b)
    return join_half(keep, swap(send, b)), [x for x in left if x != b]


def scatter_first(grad, orders):
    width = grad.shape[1] // len(orders)
    left = [b for b in all_bits() if b != 0]
    return [
        halving_step(grad[:, i * width : (i + 1) * width], left, order[0])[0].astype(jnp.bfloat16)
        for i, order in enumerate(orders)
    ]


def scatter_rest(parts, orders):
    done = []
    for part, order in zip(parts, orders):
        left = [b for b in all_bits() if b != 0 and b != order[0]]
        for b in [b for b in order if b in left] + [b for b in left if b not in order]:
            part, left = halving_step(part, left, b)
        done.append(part)
    return jnp.concatenate(done, axis=1)


def gather_vectors(shards_in):
    packed = jnp.concatenate(shards_in)
    other = swap(packed, "g")
    first = lax.axis_index("grp") == 0
    low, high = jnp.where(first, packed, other), jnp.where(first, other, packed)
    out, at = [], 0
    for v in shards_in:
        n = v.shape[0]
        out.append(jnp.concatenate([low[at : at + n], high[at : at + n]]))
        at += n
    return out


def sum_vectors(vectors):
    halves = [v.reshape(2, -1) for v in vectors]
    packed = jnp.concatenate(halves, axis=1)
    lanes = 128
    packed = packed.reshape(2, -1, lanes)
    mine = lax.axis_index("grp")
    total = lax.dynamic_index_in_dim(packed, mine, 0, False) + swap(
        lax.dynamic_index_in_dim(packed, 1 - mine, 0, False), "g"
    )
    for bit in range(lax.axis_size("rep").bit_length() - 1):
        total = total + swap(total, bit)
    total = total.reshape(-1)
    out, at = [], 0
    for h in halves:
        out.append(total[at : at + h.shape[1]])
        at += h.shape[1]
    return out


def shards(
    tokens,
    cotangent,
    tile_seq,
    seq_lens,
    attn_norm_gain,
    attn_norm_bias,
    qkv_weight,
    query_bias,
    value_bias,
    out_weight,
    out_bias,
    ffn_norm_gain,
    ffn_norm_bias,
    up_weight,
    up_bias,
    down_weight,
    down_bias,
):
    (
        attention_gain_vector,
        attention_offset_vector,
        bias_query,
        bias_value,
        bias_out,
        feedforward_gain_vector,
        feedforward_offset_vector,
        bias_up,
        bias_down,
    ) = gather_vectors(
        [
            attn_norm_gain,
            attn_norm_bias,
            query_bias,
            value_bias,
            out_bias,
            ffn_norm_gain,
            ffn_norm_bias,
            up_bias,
            down_bias,
        ]
    )
    qkv_bits, out_bits, up_bits, down_bits = (1, 0), (2, 0), (2, 1, 0), (1, 2, 0)
    weight_qkv, weight_out, weight_up, weight_down = (
        join_rows(w, spread_pieces(swap(own_piece(w, bits), "g"), bits), bits)
        for w, bits in (
            (qkv_weight, qkv_bits),
            (out_weight, out_bits),
            (up_weight, up_bits),
            (down_weight, down_bits),
        )
    )
    slots, width = tokens.shape
    heads = H
    head_dim = width // heads
    scale = head_dim ** (-0.5)
    live, allowed = slot_masks(tile_seq, seq_lens, slots)
    residual_input_rows = tokens.astype(jnp.float32)
    attention_normed_rows, attention_centred_scaled, attention_inverse_deviation = layer_norm_apply(
        residual_input_rows,
        attention_gain_vector.astype(jnp.float32),
        attention_offset_vector.astype(jnp.float32),
    )
    attn_input = attention_normed_rows.astype(jnp.bfloat16)
    projected = jnp.dot(attn_input, weight_qkv, preferred_element_type=jnp.float32)
    queries = (
        (projected[:, :width] + bias_query.astype(jnp.float32))
        .astype(jnp.bfloat16)
        .reshape(slots, heads, head_dim)
    )
    key_rows = projected[:, width : 2 * width].astype(jnp.bfloat16).reshape(slots, heads, head_dim)
    value_rows = (
        (projected[:, 2 * width :] + bias_value.astype(jnp.float32))
        .astype(jnp.bfloat16)
        .reshape(slots, heads, head_dim)
    )
    scores = (
        jnp.einsum("qhd,khd->hqk", queries, key_rows, preferred_element_type=jnp.float32) * scale
    )
    scores = jnp.where(allowed[None], scores, -1e30)
    top_score = jnp.max(scores, axis=-1, keepdims=True)
    log_total = top_score + jnp.log(jnp.sum(jnp.exp(scores - top_score), axis=-1, keepdims=True))
    probs_low = jnp.where(allowed[None], jnp.exp(scores - log_total), 0.0).astype(jnp.bfloat16)
    context = jnp.einsum("hqk,khd->qhd", probs_low, value_rows, preferred_element_type=jnp.float32)
    context = context.reshape(slots, width).astype(jnp.bfloat16)
    middle_residual_rows = (
        residual_input_rows
        + jnp.dot(context, weight_out, preferred_element_type=jnp.float32)
        + bias_out.astype(jnp.float32)
    )
    feedforward_normed_rows, feedforward_centred_scaled, feedforward_inverse_deviation = (
        layer_norm_apply(
            middle_residual_rows,
            feedforward_gain_vector.astype(jnp.float32),
            feedforward_offset_vector.astype(jnp.float32),
        )
    )
    ffn_input = feedforward_normed_rows.astype(jnp.bfloat16)
    up_sum = jnp.dot(ffn_input, weight_up, preferred_element_type=jnp.float32) + bias_up.astype(
        jnp.float32
    )
    hidden = gelu_tanh(up_sum).astype(jnp.bfloat16)
    ffn_out = jnp.dot(hidden, weight_down, preferred_element_type=jnp.float32)
    final_resid = middle_residual_rows + ffn_out + bias_down.astype(jnp.float32)
    out_grad = cotangent.astype(jnp.float32) * live[:, None].astype(jnp.float32)
    out_low = out_grad.astype(jnp.bfloat16)
    grad_down_bias = jnp.sum(out_grad, axis=0)
    grad_down = outer_sum(hidden, out_low)
    hidden_grad = times_transpose(out_low, weight_down)
    up_grad = hidden_grad * gelu_slope(up_sum)
    grad_up_bias = jnp.sum(up_grad, axis=0)
    up_low = up_grad.astype(jnp.bfloat16)
    grad_up = outer_sum(ffn_input, up_low)
    normed_rows_gradient = times_transpose(up_low, weight_up)
    keep_down, send_down = core_halves(grad_down)
    keep_up, send_up = core_halves(grad_up)
    normed_rows_gradient, send_down, send_up = lax.optimization_barrier(
        (normed_rows_gradient, send_down, send_up)
    )
    recv_down, recv_up = swap(send_down, 0), swap(send_up, 0)
    feedforward_backward_result, feedforward_gain_gradient, feedforward_offset_gradient = (
        norm_backward_pass(
            normed_rows_gradient,
            feedforward_centred_scaled,
            feedforward_inverse_deviation,
            feedforward_gain_vector.astype(jnp.float32),
        )
    )
    resid_grad = out_grad + feedforward_backward_result
    grad_out_bias = jnp.sum(resid_grad, axis=0)
    resid_low = resid_grad.astype(jnp.bfloat16)
    grad_out = outer_sum(context, resid_low)
    context_grad = (
        times_transpose(resid_low, weight_out).astype(jnp.bfloat16).reshape(slots, heads, head_dim)
    )
    again_scores = (
        jnp.einsum("qhd,khd->hqk", queries, key_rows, preferred_element_type=jnp.float32) * scale
    )
    attn_probs = jnp.where(
        allowed[None], jnp.exp(jnp.where(allowed[None], again_scores, -1e30) - log_total), 0.0
    )
    again_low = attn_probs.astype(jnp.bfloat16)
    half_down = join_half(keep_down, recv_down).astype(jnp.bfloat16)
    half_up = join_half(keep_up, recv_up).astype(jnp.bfloat16)
    context_grad, half_down, half_up = lax.optimization_barrier((context_grad, half_down, half_up))
    down_orders, up_orders = (("g", 1, 2, 3), (1, 2, "g", 3)), ((2, "g", 1, 3), ("g", 2, 1, 3))
    parts_down = scatter_first(half_down, down_orders)
    parts_up = scatter_first(half_up, up_orders)
    value_grad = jnp.einsum(
        "hqk,qhd->khd", again_low, context_grad, preferred_element_type=jnp.float32
    )
    prob_grad = jnp.einsum(
        "qhd,khd->hqk", context_grad, value_rows, preferred_element_type=jnp.float32
    )
    row_dot = jnp.sum(attn_probs * prob_grad, axis=-1, keepdims=True)
    score_grad = (scale * attn_probs * (prob_grad - row_dot)).astype(jnp.bfloat16)
    query_grad = jnp.einsum(
        "hqk,khd->qhd", score_grad, key_rows, preferred_element_type=jnp.float32
    ).reshape(slots, width)
    key_grad = jnp.einsum(
        "hqk,qhd->khd", score_grad, queries, preferred_element_type=jnp.float32
    ).reshape(slots, width)
    value_grad = value_grad.reshape(slots, width)
    grad_query_bias = jnp.sum(query_grad, axis=0)
    grad_value_bias = jnp.sum(value_grad, axis=0)
    proj_grad = jnp.concatenate([query_grad, key_grad, value_grad], axis=1).astype(jnp.bfloat16)
    grad_qkv = outer_sum(attn_input, proj_grad)
    normed_backward_result = times_transpose(proj_grad, weight_qkv)
    attention_backward_result, attention_gain_gradient, attention_offset_gradient = (
        norm_backward_pass(
            normed_backward_result,
            attention_centred_scaled,
            attention_inverse_deviation,
            attention_gain_vector.astype(jnp.float32),
        )
    )
    input_grad = resid_grad + attention_backward_result
    keep_out, send_out = core_halves(grad_out)
    keep_qkv, send_qkv = core_halves(grad_qkv)
    half_out = join_half(keep_out, swap(send_out, 0)).astype(jnp.bfloat16)
    half_qkv = join_half(keep_qkv, swap(send_qkv, 0)).astype(jnp.bfloat16)
    parts_down, parts_up, half_out, half_qkv = lax.optimization_barrier(
        (parts_down, parts_up, half_out, half_qkv)
    )
    grad_down = scatter_rest(parts_down, down_orders)
    grad_up = scatter_rest(parts_up, up_orders)
    out_orders = ((1, 2, "g", 3),)
    grad_out = scatter_rest(scatter_first(half_out, out_orders), out_orders)
    qkv_orders = (("g", 1, 2, 3), (1, 2, "g", 3), (2, "g", 1, 3))
    grad_qkv = scatter_rest(scatter_first(half_qkv, qkv_orders), qkv_orders)
    (
        attention_gain_gradient,
        attention_offset_gradient,
        grad_query_bias,
        grad_value_bias,
        grad_out_bias,
        feedforward_gain_gradient,
        feedforward_offset_gradient,
        grad_up_bias,
        grad_down_bias,
    ) = sum_vectors(
        [
            attention_gain_gradient,
            attention_offset_gradient,
            grad_query_bias,
            grad_value_bias,
            grad_out_bias,
            feedforward_gain_gradient,
            feedforward_offset_gradient,
            grad_up_bias,
            grad_down_bias,
        ]
    )
    return (
        middle_residual_rows.astype(jnp.bfloat16),
        final_resid.astype(jnp.bfloat16),
        input_grad,
        attention_gain_gradient,
        attention_offset_gradient,
        grad_qkv,
        grad_query_bias,
        grad_value_bias,
        grad_out,
        grad_out_bias,
        feedforward_gain_gradient,
        feedforward_offset_gradient,
        grad_up,
        grad_up_bias,
        grad_down,
        grad_down_bias,
    )


def solution(mesh):
    return jax.shard_map(
        shards,
        mesh=mesh,
        in_specs=(
            P(("rep", "grp"), None),
            P(("rep", "grp"), None),
            P(("rep", "grp")),
            P(),
            P("grp"),
            P("grp"),
            P("grp", None),
            P("grp"),
            P("grp"),
            P("grp", None),
            P("grp"),
            P("grp"),
            P("grp"),
            P("grp", None),
            P("grp"),
            P("grp", None),
            P("grp"),
        ),
        out_specs=(
            P(("rep", "grp"), None),
            P(("rep", "grp"), None),
            P(("rep", "grp"), None),
            P("grp"),
            P("grp"),
            P(("grp", "rep"), None),
            P("grp"),
            P("grp"),
            P(("grp", "rep"), None),
            P("grp"),
            P("grp"),
            P("grp"),
            P(("grp", "rep"), None),
            P("grp"),
            P(("grp", "rep"), None),
            P("grp"),
        ),
        check_vma=False,
    )
```
